32 devices in a mesh: dom: 8 (over z, core), grp: 4 (over y, x).
Axes of the slice: x: 2, y: 2, z: 4, core: 2. Of those that a mesh axis runs over, the one named last changes fastest.
Arguments:
- feats: bfloat16 [8192, 256], P(('dom', 'grp')), may hold values from -6 to 6
- w_self: bfloat16 [256, 256], replicated, may hold values from -0.375 to 0.375
- w_neigh: bfloat16 [256, 256], replicated, may hold values from -0.375 to 0.375
- local_tiles: bfloat16 [64, 3, 128, 128], P(('dom', 'grp')), may hold values from -0.15625 to 0.15625
- local_cols: int32 [64, 3], P(('dom', 'grp')), may hold values from 0 to 7, as said below
- cut_tiles: bfloat16 [64, 10, 128, 128], P(('dom', 'grp')), may hold values from -0.15625 to 0.15625
- cut_src: int32 [64, 10], P(('dom', 'grp')), may hold values from 0 to 7, as said below
- send_block: int32 [32, 8], P(('dom', 'grp')), may hold values from 0 to 1
- send_live: int32 [32, 8], P(('dom', 'grp')), may hold values from 0 to 1, as said below
- cotangent: bfloat16 [8192, 256], P(('dom', 'grp')), may hold values from -0.0625 to 0.0625
Outputs:
- layer_out: bfloat16 [8192, 256], P(('dom', 'grp'))
- grad_self: float32 [256, 256], replicated
- grad_neigh: float32 [256, 256], replicated
The draws below stay inside these ranges and needn't reach their ends.
Inputs may be any that keep to these rules, and one draw needn't show every extreme that they name: `local_cols`: the 3 column blocks of one row block are distinct. `cut_src`: 0 marks an empty slot; the share of filled slots differs from partition to partition. send_live[e, p] is 1 exactly when some row block of device p * 4 + g (g the position of e) has a cut slot with offset naming e's partition; it is 0 where p is e's own partition.
All inputs are finite; a program needn't handle non-finite values.
Results may differ from the reference program's by a relative error of at most 0.0056.
Values may be sent and summed in bfloat16 or wider, within the bound.
A program may use at most 64 MiB of HBM per device.

```python
import jax
import jax.numpy as jnp
from jax import lax

D = 256
BLOCK = 128
RB = 2
KC = 10
PBLOCKS = 8
K = 3
NODES = 8192
N_DOM = 8
N_GRP = 4


def draw_local_cols(key, part):
    keys = jax.random.split(key, NODES // BLOCK)

    def pick_row(one_key):
        return jax.random.permutation(one_key, PBLOCKS)[:K]
    return jax.vmap(pick_row)(keys).astype(jnp.int32)


def cut_plan(key):
    base = jax.random.fold_in(key, 7101)
    level_key = jax.random.fold_in(base, 1)
    top_key = jax.random.fold_in(base, 2)
    slot_key = jax.random.fold_in(base, 3)
    first_key = jax.random.fold_in(base, 4)
    second_key = jax.random.fold_in(base, 5)
    levels = jax.random.randint(level_key, (N_DOM,), 1, 5)
    top_part = jax.random.randint(top_key, (), 0, N_DOM)
    levels = jnp.where(jnp.arange(N_DOM, dtype=jnp.int32) == top_part, 4, levels).astype(jnp.int32)
    row_count = NODES // BLOCK
    row_part = (jnp.arange(row_count, dtype=jnp.int32) // (N_GRP * RB)).astype(jnp.int32)
    slot_roll = jax.random.randint(slot_key, (row_count, KC), 0, 4)
    filled = slot_roll < levels[row_part][:, None]
    first = jax.random.randint(first_key, (row_count, KC), 0, N_DOM - 1)
    second = jax.random.randint(second_key, (row_count, KC), 0, N_DOM - 1)
    offsets = jnp.minimum(first, second) + 1
    cut_offsets = jnp.where(filled, offsets, 0).astype(jnp.int32)
    grouped = cut_offsets.reshape(N_DOM, N_GRP, RB * KC)
    src_part = jnp.arange(N_DOM, dtype=jnp.int32)[:, None, None, None]
    dst_part = jnp.arange(N_DOM, dtype=jnp.int32)[None, None, :, None]
    wanted = (src_part - dst_part) % N_DOM
    reads = grouped.transpose(1, 0, 2)[None, :, :, :]
    hits = jnp.logical_and(reads == wanted, reads != 0)
    live = jnp.any(hits, axis=3).astype(jnp.int32)
    return (cut_offsets, live.reshape(N_DOM * N_GRP, N_DOM))


def draw_cut_src(key, part):
    return cut_plan(key)[0]


def draw_send_live(key, part):
    return cut_plan(key)[1]


def plant(entries, stream_key, smallest, high):
    longest = entries.shape.index(max(entries.shape))
    spots = []
    for shift in (0, 1):
        where = [jax.random.randint(jax.random.fold_in(stream_key, axis), (), 0, length) for axis, length in enumerate(entries.shape)]
        where[longest] = (where[longest] + shift) % entries.shape[longest]
        spots.append(tuple(where))
    return entries.at[spots[0]].set(smallest).at[spots[1]].set(high)


def steps_of(key, dims, pieces, least, top_value):
    gain, own = 1.0, jax.random.fold_in(key, 6)
    for dim, parts in pieces:
        draws = jnp.exp(jax.random.uniform(jax.random.fold_in(own, dim), (parts,), jnp.float32, least / len(pieces), top_value / len(pieces)))
        gain = gain * jnp.repeat(draws, dims[dim] // parts).reshape([-1 if axis == dim else 1 for axis in range(len(dims))])
    return gain


def gaussian(own_key, extent, spread, reach, cuts=(), held_as=jnp.bfloat16):
    array = spread * jax.random.normal(own_key, extent, jnp.float32)
    if cuts:
        array = array * steps_of(own_key, extent, cuts, -0.22, 0.18)
    return jnp.clip(array, -reach, reach).astype(held_as)


def setup_inputs(seed: int = 0) -> dict:
    splits = jax.random.split(jax.random.key(seed), 11)
    feats = gaussian(splits[0], (NODES, D), 1.0, 6.0, ((0, 32),))
    w_self = gaussian(splits[1], (D, D), D ** -0.5, 0.375)
    w_neigh = gaussian(splits[2], (D, D), D ** -0.5, 0.375)
    local_tiles = gaussian(splits[3], (NODES // BLOCK, K, BLOCK, BLOCK), (1.0 / (BLOCK * (K + KC)) ** 0.5), 0.15625, ((0, 32),))
    local_cols = draw_local_cols(jax.random.fold_in(splits[10], 71), 0)
    cut_tiles = gaussian(splits[5], (NODES // BLOCK, KC, BLOCK, BLOCK), (1.0 / (BLOCK * (K + KC)) ** 0.5), 0.15625, ((0, 32),))
    cut_src = draw_cut_src(jax.random.fold_in(splits[10], 71), 0)
    send_block = plant(jax.random.randint(splits[7], (N_DOM * N_GRP, N_DOM), 0, RB), jax.random.fold_in(splits[7], 1), 0, RB - 1).astype(jnp.int32)
    send_live = draw_send_live(jax.random.fold_in(splits[10], 71), 0)
    cotangent = gaussian(splits[9], (NODES, D), (1.0 / NODES ** 0.5), 0.0625, ((0, 32),))
    return {"feats": feats, "w_self": w_self, "w_neigh": w_neigh, "local_tiles": local_tiles, "local_cols": local_cols, "cut_tiles": cut_tiles, "cut_src": cut_src, "send_block": send_block, "send_live": send_live, "cotangent": cotangent}


def reference(feats, w_self, w_neigh, local_tiles, local_cols, cut_tiles, cut_src, send_block, send_live, cotangent):
    feature_blocks = feats.reshape(N_DOM * N_GRP * RB, BLOCK, D)

    def aggregate_device(device):
        part_id = device // N_GRP
        group_id = device % N_GRP
        tiles_here = lax.dynamic_slice_in_dim(local_tiles, device * RB, RB, 0)
        cols_here = lax.dynamic_slice_in_dim(local_cols, device * RB, RB, 0)
        global_ids = (part_id * PBLOCKS + cols_here).astype(jnp.int32)
        chosen = feature_blocks[global_ids].astype(jnp.float32)
        total = jnp.einsum("rkij,rkjf->rif", tiles_here.astype(jnp.float32), chosen)
        cut_here = lax.dynamic_slice_in_dim(cut_tiles, device * RB, RB, 0)
        offsets = lax.dynamic_slice_in_dim(cut_src, device * RB, RB, 0)
        source = (part_id + offsets) % N_DOM
        source_dev = (source * N_GRP + group_id).astype(jnp.int32)
        sent_block = send_block[source_dev, part_id]
        alive = send_live[source_dev, part_id].astype(jnp.float32)
        remote = feature_blocks[(source_dev * RB + sent_block).astype(jnp.int32)].astype(jnp.float32)
        remote = remote * alive[:, :, None, None]
        total = total + jnp.einsum("rkij,rkjf->rif", cut_here.astype(jnp.float32), remote)
        return total.reshape(RB * BLOCK, D)

    devices = jnp.arange(N_DOM * N_GRP, dtype=jnp.int32)
    agg = lax.map(aggregate_device, devices).reshape(NODES, D).astype(jnp.bfloat16)
    preact = jnp.dot(feats, w_self, preferred_element_type=jnp.float32) + jnp.dot(agg, w_neigh, preferred_element_type=jnp.float32)
    sigmoid = jax.nn.sigmoid(preact)
    layer_out = (preact * sigmoid).astype(jnp.bfloat16)
    grad_pre = (cotangent.astype(jnp.float32) * sigmoid * (1.0 + preact * (1.0 - sigmoid))).astype(jnp.bfloat16)
    grad_self = jnp.dot(feats.T, grad_pre, preferred_element_type=jnp.float32)
    grad_neigh = jnp.dot(agg.T, grad_pre, preferred_element_type=jnp.float32)
    return layer_out, grad_self, grad_neigh
```

```python
import functools

import jax
import jax.numpy as jnp
from jax import lax
from jax.experimental import pallas as pl
from jax.experimental.pallas import tpu as pltpu
from jax.sharding import PartitionSpec as P

MESH = pl.DeviceIdType.MESH
PACK = 16


def f32_dot(a, b):
    return jnp.dot(a, b, preferred_element_type=jnp.float32)


def kernel(
    n_dom,
    n_grp,
    cols_ref,
    src_ref,
    block_ref,
    live_ref,
    feats_ref,
    w_self_ref,
    w_neigh_ref,
    local_ref,
    cut_ref,
    cot_ref,
    out_ref,
    grad_ref,
    near,
    outgoing,
    far,
    acc,
    part,
    part_low,
    sums1,
    mid,
    sums2,
    near_send,
    near_recv,
    far_send,
    far_recv,
    s1_send,
    s1_recv,
    s2_send,
    s2_recv,
    s3_send,
    s3_recv,
    s4_send,
    s4_recv,
):
    row_blocks, local_slots, block, _ = local_ref.shape
    cut_slots = cut_ref.shape[1]
    features = feats_ref.shape[2]
    me_d, me_g = lax.axis_index("dom"), lax.axis_index("grp")
    dom_peer = [lax.rem(me_d + o, n_dom) for o in range(n_dom)]
    grp_peer = [lax.rem(me_g + o, n_grp) for o in range(n_grp)]

    def remote(src, dst, send, recv, o, axis):
        peer = dom_peer[o] if axis == "dom" else grp_peer[o]
        return pltpu.make_async_remote_copy(
            src_ref=src,
            dst_ref=dst,
            send_sem=send.at[o],
            recv_sem=recv.at[o],
            device_id={axis: peer},
            device_id_type=MESH,
        )

    barrier = pltpu.get_barrier_semaphore()
    for o in range(1, n_dom):
        pl.semaphore_signal(barrier, inc=1, device_id={"dom": dom_peer[o]}, device_id_type=MESH)
    for o in range(1, n_grp):
        pl.semaphore_signal(barrier, inc=1, device_id={"grp": grp_peer[o]}, device_id_type=MESH)

    for o in range(n_dom):
        alive = live_ref[0, dom_peer[o]].astype(jnp.float32)
        chosen = feats_ref[block_ref[0, dom_peer[o]]].astype(jnp.float32)
        target = far if o == 0 else outgoing
        target[o] = (chosen * alive).astype(jnp.bfloat16)
    pl.semaphore_wait(barrier, n_dom + n_grp - 2)

    far_copies = [
        remote(outgoing.at[o], far.at[o], far_send, far_recv, o, "dom") for o in range(1, n_dom)
    ]
    near_copies = [
        remote(
            feats_ref,
            near.at[pl.ds(o * row_blocks, row_blocks)],
            near_send,
            near_recv,
            o,
            "grp",
        )
        for o in range(1, n_grp)
    ]
    for copy in far_copies + near_copies:
        copy.start()

    near[0:row_blocks] = feats_ref[...]
    for copy in near_copies:
        copy.wait()
    for b in range(row_blocks):
        total = jnp.zeros((block, features), jnp.float32)
        for k in range(local_slots):
            col = cols_ref[b, k]
            owner = lax.div(col, row_blocks)
            slot = lax.rem(me_g - owner + n_grp, n_grp)
            where = slot * row_blocks + lax.rem(col, row_blocks)
            total = total + f32_dot(local_ref[b, k], near[where])
        acc[b] = total

    for copy in far_copies:
        copy.wait()
    grads_own = jnp.zeros((features, features), jnp.float32)
    grads_agg = jnp.zeros((features, features), jnp.float32)
    for b in range(row_blocks):
        total = acc[b]
        for k in range(cut_slots):
            slot = lax.rem(n_dom - src_ref[b, k], n_dom)
            total = total + f32_dot(cut_ref[b, k], far[slot])
        agg = total.astype(jnp.bfloat16)
        own = feats_ref[b]
        preact = f32_dot(own, w_self_ref[...]) + f32_dot(agg, w_neigh_ref[...])
        sig = jax.nn.sigmoid(preact)
        out_ref[b] = (preact * sig).astype(jnp.bfloat16)
        grad_pre = (
            cot_ref[b].astype(jnp.float32) * sig * (1.0 + preact * (1.0 - sig))
        ).astype(jnp.bfloat16)
        dims = (((0,), (0,)), ((), ()))
        grads_own = grads_own + lax.dot_general(
            own, grad_pre, dims, preferred_element_type=jnp.float32
        )
        grads_agg = grads_agg + lax.dot_general(
            agg, grad_pre, dims, preferred_element_type=jnp.float32
        )
    part[0:features] = grads_own
    part[features : 2 * features] = grads_agg
    part_low[0:features] = grads_own.astype(jnp.bfloat16)
    part_low[features : 2 * features] = grads_agg.astype(jnp.bfloat16)

    rows = 2 * features // n_grp
    mine = pl.ds(pl.multiple_of(me_g * rows, rows), rows)
    copies = [
        remote(
            part_low.at[pl.ds(pl.multiple_of(grp_peer[o] * rows, rows), rows)],
            sums1.at[o],
            s1_send,
            s1_recv,
            o,
            "grp",
        )
        for o in range(1, n_grp)
    ]
    for copy in copies:
        copy.start()
    total = part[mine]
    for o, copy in enumerate(copies, 1):
        copy.wait()
        total = total + sums1[o].astype(jnp.float32)
    mid[...] = total

    if rows % (PACK * n_dom) == 0:
        piece = rows // n_dom
        here = pl.ds(pl.multiple_of(me_d * piece, piece), piece)
        copies = [
            remote(
                mid.at[pl.ds(pl.multiple_of(dom_peer[o] * piece, piece), piece)],
                sums2.at[o],
                s2_send,
                s2_recv,
                o,
                "dom",
            )
            for o in range(1, n_dom)
        ]
        for copy in copies:
            copy.start()
        total = mid[here]
        for o, copy in enumerate(copies, 1):
            copy.wait()
            total = total + sums2[o]
        spot = pl.ds(pl.multiple_of(me_g * rows + me_d * piece, piece), piece)
        grad_ref[spot] = total.astype(jnp.bfloat16)
        copies = [
            remote(grad_ref.at[spot], grad_ref.at[spot], s3_send, s3_recv, o, "dom")
            for o in range(1, n_dom)
        ]
        for copy in copies:
            copy.start()
        for copy in copies:
            copy.wait()
    else:
        copies = [
            remote(mid, sums2.at[o], s2_send, s2_recv, o, "dom") for o in range(1, n_dom)
        ]
        for copy in copies:
            copy.start()
        total = mid[...]
        for o, copy in enumerate(copies, 1):
            copy.wait()
            total = total + sums2[o]
        grad_ref[mine] = total.astype(jnp.bfloat16)

    copies = [
        remote(grad_ref.at[mine], grad_ref.at[mine], s4_send, s4_recv, o, "grp")
        for o in range(1, n_grp)
    ]
    for copy in copies:
        copy.start()
    for copy in copies:
        copy.wait()


def body(
    feats,
    w_self,
    w_neigh,
    local_tiles,
    local_cols,
    cut_tiles,
    cut_src,
    send_block,
    send_live,
    cotangent,
):
    row_blocks, _, block, _ = local_tiles.shape
    features = feats.shape[1]
    n_dom, n_grp = lax.axis_size("dom"), lax.axis_size("grp")
    blocks = (row_blocks, block, features)
    rows = 2 * features // n_grp
    piece = rows // n_dom if rows % (PACK * n_dom) == 0 else rows
    dma = pltpu.SemaphoreType.DMA
    smem = pl.BlockSpec(memory_space=pltpu.SMEM)
    vmem = pl.BlockSpec(memory_space=pltpu.VMEM)
    out, grads = pl.pallas_call(
        functools.partial(kernel, n_dom, n_grp),
        out_shape=(
            jax.ShapeDtypeStruct(blocks, jnp.bfloat16),
            jax.ShapeDtypeStruct((2 * features, features), jnp.bfloat16),
        ),
        in_specs=[smem] * 4 + [vmem] * 6,
        out_specs=(vmem, vmem),
        scratch_shapes=[
            pltpu.VMEM((n_grp * row_blocks, block, features), jnp.bfloat16),
            pltpu.VMEM((n_dom, block, features), jnp.bfloat16),
            pltpu.VMEM((n_dom, block, features), jnp.bfloat16),
            pltpu.VMEM(blocks, jnp.float32),
            pltpu.VMEM((2 * features, features), jnp.float32),
            pltpu.VMEM((2 * features, features), jnp.bfloat16),
            pltpu.VMEM((n_grp, rows, features), jnp.bfloat16),
            pltpu.VMEM((rows, features), jnp.float32),
            pltpu.VMEM((n_dom, piece, features), jnp.float32),
        ]
        + [dma((n_grp,))] * 2
        + [dma((n_dom,))] * 2
        + [dma((n_grp,))] * 2
        + [dma((n_dom,))] * 4
        + [dma((n_grp,))] * 2,
        compiler_params=pltpu.CompilerParams(
            collective_id=0, has_side_effects=True, vmem_limit_bytes=32 * 2**20
        ),
    )(
        local_cols,
        cut_src,
        send_block,
        send_live,
        feats.reshape(blocks),
        w_self,
        w_neigh,
        local_tiles,
        cut_tiles,
        cotangent.reshape(blocks),
    )
    summed = grads.astype(jnp.float32)
    return (out.reshape(feats.shape), summed[:features], summed[features:])


def solution(mesh):
    return jax.shard_map(
        body,
        mesh=mesh,
        in_specs=(
            P(("dom", "grp"), None),
            P(),
            P(),
            P(("dom", "grp"), None, None, None),
            P(("dom", "grp"), None),
            P(("dom", "grp"), None, None, None),
            P(("dom", "grp"), None),
            P(("dom", "grp"), None),
            P(("dom", "grp"), None),
            P(("dom", "grp"), None),
        ),
        out_specs=(P(("dom", "grp"), None), P(), P()),
        check_vma=False,
    )
```

```python
import functools

import jax
import jax.numpy as jnp
from jax import lax
from jax.experimental import pallas as pl
from jax.experimental.pallas import tpu as pltpu
from jax.sharding import PartitionSpec as P

MESH = pl.DeviceIdType.MESH
PACK = 16


def f32_dot(a, b):
    return jnp.dot(a, b, preferred_element_type=jnp.float32)


def kernel(
    n_dom,
    n_grp,
    cols_hbm,
    src_hbm,
    block_hbm,
    live_hbm,
    feats_hbm,
    w_self_hbm,
    w_neigh_hbm,
    local_hbm,
    cut_hbm,
    cot_hbm,
    out_ref,
    grad_ref,
    cols_ref,
    src_ref,
    block_ref,
    live_ref,
    w_self_ref,
    w_neigh_ref,
    local_ref,
    cut_ref,
    cot_ref,
    feats_ref,
    near,
    outgoing,
    far,
    acc,
    pre,
    part,
    part_low,
    sums1,
    mid,
    sums2,
    load_sem,
    near_send,
    near_recv,
    far_send,
    far_recv,
    s1_send,
    s1_recv,
    s2_send,
    s2_recv,
    s3_send,
    s3_recv,
    s4_send,
    s4_recv,
):
    row_blocks, local_slots, block, _ = local_ref.shape
    cut_slots = cut_ref.shape[1]
    features = w_self_ref.shape[0]
    halves, _, width = part.shape
    me_d, me_g = lax.axis_index("dom"), lax.axis_index("grp")
    dom_peer = [lax.rem(me_d + o, n_dom) for o in range(n_dom)]
    grp_peer = [lax.rem(me_g + o, n_grp) for o in range(n_grp)]

    def remote(src, dst, send, recv, o, axis):
        peer = dom_peer[o] if axis == "dom" else grp_peer[o]
        return pltpu.make_async_remote_copy(
            src_ref=src,
            dst_ref=dst,
            send_sem=send,
            recv_sem=recv,
            device_id={axis: peer},
            device_id_type=MESH,
        )

    def begin(copies):
        for copy in copies:
            copy.start()
        return copies

    loads = begin(
        [
            pltpu.make_async_copy(src, dst, load_sem.at[i])
            for i, (src, dst) in enumerate(
                (
                    (block_hbm, block_ref),
                    (live_hbm, live_ref),
                    (feats_hbm, feats_ref),
                    (feats_hbm, near.at[pl.ds(0, row_blocks)]),
                    (cols_hbm, cols_ref),
                    (src_hbm, src_ref),
                    (w_self_hbm, w_self_ref),
                    (local_hbm, local_ref),
                    (cut_hbm, cut_ref),
                    (w_neigh_hbm, w_neigh_ref),
                    (cot_hbm, cot_ref),
                )
            )
        ]
    )
    barrier = pltpu.get_barrier_semaphore()
    for o in range(1, n_dom):
        pl.semaphore_signal(barrier, inc=1, device_id={"dom": dom_peer[o]}, device_id_type=MESH)
    for o in range(1, n_grp):
        pl.semaphore_signal(barrier, inc=1, device_id={"grp": grp_peer[o]}, device_id_type=MESH)
    for load in loads[:3]:
        load.wait()

    for o in range(n_dom):
        alive = live_ref[0, dom_peer[o]].astype(jnp.float32)
        chosen = feats_ref[block_ref[0, dom_peer[o]]].astype(jnp.float32)
        target = far if o == 0 else outgoing
        target[o] = (chosen * alive).astype(jnp.bfloat16)
    pl.semaphore_wait(barrier, n_dom + n_grp - 2)

    far_copies = begin(
        [
            remote(outgoing.at[o], far.at[o], far_send.at[o], far_recv.at[o], o, "dom")
            for o in range(1, n_dom)
        ]
    )
    near_copies = begin(
        [
            remote(
                feats_ref,
                near.at[pl.ds(o * row_blocks, row_blocks)],
                near_send.at[o],
                near_recv.at[o],
                o,
                "grp",
            )
            for o in range(1, n_grp)
        ]
    )

    for load in loads[3:]:
        load.wait()
    for b in range(row_blocks):
        pre[b] = f32_dot(feats_ref[b], w_self_ref[...])
    for copy in near_copies:
        copy.wait()
    for b in range(row_blocks):
        total = jnp.zeros((block, features), jnp.float32)
        for k in range(local_slots):
            col = cols_ref[b, k]
            owner = lax.div(col, row_blocks)
            slot = lax.rem(me_g - owner + n_grp, n_grp)
            where = slot * row_blocks + lax.rem(col, row_blocks)
            total = total + f32_dot(local_ref[b, k], near[where])
        acc[b] = total

    for copy in far_copies:
        copy.wait()
    grads_own = jnp.zeros((features, features), jnp.float32)
    grads_agg = jnp.zeros((features, features), jnp.float32)
    for b in range(row_blocks):
        total = acc[b]
        for k in range(cut_slots):
            slot = lax.rem(n_dom - src_ref[b, k], n_dom)
            total = total + f32_dot(cut_ref[b, k], far[slot])
        agg = total.astype(jnp.bfloat16)
        own = feats_ref[b]
        preact = pre[b] + f32_dot(agg, w_neigh_ref[...])
        sig = jax.nn.sigmoid(preact)
        out_ref[b] = (preact * sig).astype(jnp.bfloat16)
        grad_pre = (
            cot_ref[b].astype(jnp.float32) * sig * (1.0 + preact * (1.0 - sig))
        ).astype(jnp.bfloat16)
        dims = (((0,), (0,)), ((), ()))
        grads_own = grads_own + lax.dot_general(
            own, grad_pre, dims, preferred_element_type=jnp.float32
        )
        grads_agg = grads_agg + lax.dot_general(
            agg, grad_pre, dims, preferred_element_type=jnp.float32
        )

    rows = 2 * features // n_grp
    mine = pl.ds(pl.multiple_of(me_g * rows, rows), rows)
    split = rows % (PACK * n_dom) == 0
    piece = rows // n_dom if split else rows
    here = pl.ds(pl.multiple_of(me_d * piece, piece), piece) if split else pl.ds(0, rows)
    spot = (
        pl.ds(pl.multiple_of(me_g * rows + me_d * piece, piece), piece) if split else mine
    )

    columns = [pl.ds(h * width, width) for h in range(halves)]

    first = []
    for h in range(halves):
        cut = slice(h * width, (h + 1) * width)
        part[h, 0:features] = grads_own[:, cut]
        part[h, features : 2 * features] = grads_agg[:, cut]
        part_low[h, 0:features] = grads_own[:, cut].astype(jnp.bfloat16)
        part_low[h, features : 2 * features] = grads_agg[:, cut].astype(jnp.bfloat16)
        first.append(
            begin(
                [
                    remote(
                        part_low.at[h, pl.ds(pl.multiple_of(grp_peer[o] * rows, rows), rows)],
                        sums1.at[h, o],
                        s1_send.at[h, o],
                        s1_recv.at[h, o],
                        o,
                        "grp",
                    )
                    for o in range(1, n_grp)
                ]
            )
        )
    second = []
    for h in range(halves):
        total = part[h, mine]
        for o, copy in enumerate(first[h], 1):
            copy.wait()
            total = total + sums1[h, o].astype(jnp.float32)
        mid[h] = total
        second.append(
            begin(
                [
                    remote(
                        mid.at[
                            h,
                            pl.ds(pl.multiple_of(dom_peer[o] * piece, piece), piece)
                            if split
                            else pl.ds(0, rows),
                        ],
                        sums2.at[h, o],
                        s2_send.at[h, o],
                        s2_recv.at[h, o],
                        o,
                        "dom",
                    )
                    for o in range(1, n_dom)
                ]
            )
        )
    third = []
    for h in range(halves):
        total = mid[h, here]
        for o, copy in enumerate(second[h], 1):
            copy.wait()
            total = total + sums2[h, o]
        grad_ref[spot, columns[h]] = total.astype(jnp.bfloat16)
        if split:
            third.append(
                begin(
                    [
                        remote(
                            grad_ref.at[spot, columns[h]],
                            grad_ref.at[spot, columns[h]],
                            s3_send.at[h, o],
                            s3_recv.at[h, o],
                            o,
                            "dom",
                        )
                        for o in range(1, n_dom)
                    ]
                )
            )
    fourth = []
    for h in range(halves):
        if split:
            for copy in third[h]:
                copy.wait()
        fourth += begin(
            [
                remote(
                    grad_ref.at[mine, columns[h]],
                    grad_ref.at[mine, columns[h]],
                    s4_send.at[h, o],
                    s4_recv.at[h, o],
                    o,
                    "grp",
                )
                for o in range(1, n_grp)
            ]
        )
    for copy in fourth:
        copy.wait()


def body(
    feats,
    w_self,
    w_neigh,
    local_tiles,
    local_cols,
    cut_tiles,
    cut_src,
    send_block,
    send_live,
    cotangent,
):
    row_blocks, _, block, _ = local_tiles.shape
    features = feats.shape[1]
    n_dom, n_grp = lax.axis_size("dom"), lax.axis_size("grp")
    blocks = (row_blocks, block, features)
    rows = 2 * features // n_grp
    piece = rows // n_dom if rows % (PACK * n_dom) == 0 else rows
    halves = 2
    width = features // halves
    dma = pltpu.SemaphoreType.DMA
    hbm = pl.BlockSpec(memory_space=pltpu.HBM)
    vmem = pl.BlockSpec(memory_space=pltpu.VMEM)
    out, grads = pl.pallas_call(
        functools.partial(kernel, n_dom, n_grp),
        out_shape=(
            jax.ShapeDtypeStruct(blocks, jnp.bfloat16),
            jax.ShapeDtypeStruct((2 * features, features), jnp.bfloat16),
        ),
        in_specs=[hbm] * 10,
        out_specs=(vmem, vmem),
        scratch_shapes=[
            pltpu.SMEM(local_cols.shape, jnp.int32),
            pltpu.SMEM(cut_src.shape, jnp.int32),
            pltpu.SMEM(send_block.shape, jnp.int32),
            pltpu.SMEM(send_live.shape, jnp.int32),
            pltpu.VMEM(w_self.shape, jnp.bfloat16),
            pltpu.VMEM(w_neigh.shape, jnp.bfloat16),
            pltpu.VMEM(local_tiles.shape, jnp.bfloat16),
            pltpu.VMEM(cut_tiles.shape, jnp.bfloat16),
            pltpu.VMEM(blocks, jnp.bfloat16),
            pltpu.VMEM(blocks, jnp.bfloat16),
            pltpu.VMEM((n_grp * row_blocks, block, features), jnp.bfloat16),
            pltpu.VMEM((n_dom, block, features), jnp.bfloat16),
            pltpu.VMEM((n_dom, block, features), jnp.bfloat16),
            pltpu.VMEM(blocks, jnp.float32),
            pltpu.VMEM(blocks, jnp.float32),
            pltpu.VMEM((halves, 2 * features, width), jnp.float32),
            pltpu.VMEM((halves, 2 * features, width), jnp.bfloat16),
            pltpu.VMEM((halves, n_grp, rows, width), jnp.bfloat16),
            pltpu.VMEM((halves, rows, width), jnp.float32),
            pltpu.VMEM((halves, n_dom, piece, width), jnp.float32),
            dma((11,)),
        ]
        + [dma((n_grp,))] * 2
        + [dma((n_dom,))] * 2
        + [dma((halves, n_grp))] * 2
        + [dma((halves, n_dom))] * 4
        + [dma((halves, n_grp))] * 2,
        compiler_params=pltpu.CompilerParams(
            collective_id=0, has_side_effects=True, vmem_limit_bytes=60 * 2**20
        ),
    )(
        local_cols,
        cut_src,
        send_block,
        send_live,
        feats.reshape(blocks),
        w_self,
        w_neigh,
        local_tiles,
        cut_tiles,
        cotangent.reshape(blocks),
    )
    summed = grads.astype(jnp.float32)
    return (out.reshape(feats.shape), summed[:features], summed[features:])


def solution(mesh):
    return jax.shard_map(
        body,
        mesh=mesh,
        in_specs=(
            P(("dom", "grp"), None),
            P(),
            P(),
            P(("dom", "grp"), None, None, None),
            P(("dom", "grp"), None),
            P(("dom", "grp"), None, None, None),
            P(("dom", "grp"), None),
            P(("dom", "grp"), None),
            P(("dom", "grp"), None),
            P(("dom", "grp"), None),
        ),
        out_specs=(P(("dom", "grp"), None), P(), P()),
        check_vma=False,
    )
```

```python
import functools

import jax
import jax.numpy as jnp
from jax import lax
from jax.experimental import pallas as pl
from jax.experimental.pallas import tpu as pltpu
from jax.sharding import PartitionSpec as P

MESH = pl.DeviceIdType.MESH
PACK = 16
ORDERS = (("grp", "dom"), ("dom", "grp"))


def piece_rows(rows, n):
    return rows // n if rows % (PACK * n) == 0 else rows


def f32_dot(a, b):
    return jnp.dot(a, b, preferred_element_type=jnp.float32)


def kernel(
    n_dom,
    n_grp,
    cols_hbm,
    src_hbm,
    block_hbm,
    live_hbm,
    feats_hbm,
    w_self_hbm,
    w_neigh_hbm,
    local_hbm,
    cut_hbm,
    cot_hbm,
    out_ref,
    grad_ref,
    cols_ref,
    src_ref,
    block_ref,
    live_ref,
    w_self_ref,
    w_neigh_ref,
    local_ref,
    cut_ref,
    cot_ref,
    feats_ref,
    near,
    outgoing,
    far,
    acc,
    pre,
    part,
    part_low,
    sums1_a,
    sums1_b,
    mid_a,
    mid_b,
    low_a,
    low_b,
    sums2_a,
    sums2_b,
    load_sem,
    near_send,
    near_recv,
    far_send,
    far_recv,
    s1_send,
    s1_recv,
    s2_send,
    s2_recv,
    s3_send,
    s3_recv,
    s4_send,
    s4_recv,
):
    sums1, mid, mid_low = (sums1_a, sums1_b), (mid_a, mid_b), (low_a, low_b)
    sums2 = (sums2_a, sums2_b)
    row_blocks, local_slots, block, _ = local_ref.shape
    cut_slots = cut_ref.shape[1]
    features = w_self_ref.shape[0]
    width = part.shape[2]
    me_d, me_g = lax.axis_index("dom"), lax.axis_index("grp")
    dom_peer = [lax.rem(me_d + o, n_dom) for o in range(n_dom)]
    grp_peer = [lax.rem(me_g + o, n_grp) for o in range(n_grp)]

    def remote(src, dst, send, recv, o, axis):
        peer = dom_peer[o] if axis == "dom" else grp_peer[o]
        return pltpu.make_async_remote_copy(
            src_ref=src,
            dst_ref=dst,
            send_sem=send,
            recv_sem=recv,
            device_id={axis: peer},
            device_id_type=MESH,
        )

    def begin(copies):
        for copy in copies:
            copy.start()
        return copies

    loads = begin(
        [
            pltpu.make_async_copy(src, dst, load_sem.at[i])
            for i, (src, dst) in enumerate(
                (
                    (block_hbm, block_ref),
                    (live_hbm, live_ref),
                    (feats_hbm, feats_ref),
                    (feats_hbm, near.at[pl.ds(0, row_blocks)]),
                    (cols_hbm, cols_ref),
                    (src_hbm, src_ref),
                    (w_self_hbm, w_self_ref),
                    (local_hbm, local_ref),
                    (cut_hbm, cut_ref),
                    (w_neigh_hbm, w_neigh_ref),
                    (cot_hbm, cot_ref),
                )
            )
        ]
    )
    barrier = pltpu.get_barrier_semaphore()
    for o in range(1, n_dom):
        pl.semaphore_signal(barrier, inc=1, device_id={"dom": dom_peer[o]}, device_id_type=MESH)
    for o in range(1, n_grp):
        pl.semaphore_signal(barrier, inc=1, device_id={"grp": grp_peer[o]}, device_id_type=MESH)
    for load in loads[:3]:
        load.wait()

    for o in range(n_dom):
        alive = live_ref[0, dom_peer[o]].astype(jnp.float32)
        chosen = feats_ref[block_ref[0, dom_peer[o]]].astype(jnp.float32)
        target = far if o == 0 else outgoing
        target[o] = (chosen * alive).astype(jnp.bfloat16)
    pl.semaphore_wait(barrier, n_dom + n_grp - 2)

    far_copies = begin(
        [
            remote(outgoing.at[o], far.at[o], far_send.at[o], far_recv.at[o], o, "dom")
            for o in range(1, n_dom)
        ]
    )
    near_copies = begin(
        [
            remote(
                feats_ref,
                near.at[pl.ds(o * row_blocks, row_blocks)],
                near_send.at[o],
                near_recv.at[o],
                o,
                "grp",
            )
            for o in range(1, n_grp)
        ]
    )

    for load in loads[3:]:
        load.wait()
    for b in range(row_blocks):
        pre[b] = f32_dot(feats_ref[b], w_self_ref[...])
    for copy in near_copies:
        copy.wait()
    for b in range(row_blocks):
        total = jnp.zeros((block, features), jnp.float32)
        for k in range(local_slots):
            col = cols_ref[b, k]
            owner = lax.div(col, row_blocks)
            slot = lax.rem(me_g - owner + n_grp, n_grp)
            where = slot * row_blocks + lax.rem(col, row_blocks)
            total = total + f32_dot(local_ref[b, k], near[where])
        acc[b] = total

    for copy in far_copies:
        copy.wait()
    grads_own = jnp.zeros((features, features), jnp.float32)
    grads_agg = jnp.zeros((features, features), jnp.float32)
    for b in range(row_blocks):
        total = acc[b]
        for k in range(cut_slots):
            slot = lax.rem(n_dom - src_ref[b, k], n_dom)
            total = total + f32_dot(cut_ref[b, k], far[slot])
        agg = total.astype(jnp.bfloat16)
        own = feats_ref[b]
        preact = pre[b] + f32_dot(agg, w_neigh_ref[...])
        sig = jax.nn.sigmoid(preact)
        out_ref[b] = (preact * sig).astype(jnp.bfloat16)
        grad_pre = (
            cot_ref[b].astype(jnp.float32) * sig * (1.0 + preact * (1.0 - sig))
        ).astype(jnp.bfloat16)
        dims = (((0,), (0,)), ((), ()))
        grads_own = grads_own + lax.dot_general(
            own, grad_pre, dims, preferred_element_type=jnp.float32
        )
        grads_agg = grads_agg + lax.dot_general(
            agg, grad_pre, dims, preferred_element_type=jnp.float32
        )

    peers = {"grp": grp_peer, "dom": dom_peer}
    here = {"grp": me_g, "dom": me_d}
    count = {"grp": n_grp, "dom": n_dom}

    def rows_at(start, size):
        return pl.ds(pl.multiple_of(start, size), size)

    def to_peers(axis, src, dst, send, recv):
        return begin(
            [
                remote(src(o), dst(o), send.at[o], recv.at[o], o, axis)
                for o in range(1, count[axis])
            ]
        )

    flows = []
    for h, (one, two) in enumerate(ORDERS):
        rows = 2 * features // count[one]
        piece = piece_rows(rows, count[two])
        split = piece < rows
        flows.append(
            dict(
                one=one,
                two=two,
                rows=rows,
                piece=piece,
                split=split,
                columns=pl.ds(h * width, width),
                mine=rows_at(here[one] * rows, rows),
                inner=rows_at(here[two] * piece, piece) if split else pl.ds(0, rows),
                spot=rows_at(here[one] * rows + (here[two] * piece if split else 0), piece),
                sums1=sums1[h],
                mid=mid[h],
                mid_low=mid_low[h],
                sums2=sums2[h],
            )
        )

    first = []
    for h, f in enumerate(flows):
        cut = slice(h * width, (h + 1) * width)
        part[h, 0:features] = grads_own[:, cut]
        part[h, features : 2 * features] = grads_agg[:, cut]
        part_low[h, 0:features] = grads_own[:, cut].astype(jnp.bfloat16)
        part_low[h, features : 2 * features] = grads_agg[:, cut].astype(jnp.bfloat16)
        first.append(
            to_peers(
                f["one"],
                lambda o: part_low.at[h, rows_at(peers[f["one"]][o] * f["rows"], f["rows"])],
                lambda o: f["sums1"].at[o],
                s1_send.at[h],
                s1_recv.at[h],
            )
        )
    second = []
    for h, f in enumerate(flows):
        total = part[h, f["mine"]]
        for o, copy in enumerate(first[h], 1):
            copy.wait()
            total = total + f["sums1"][o].astype(jnp.float32)
        f["mid"][...] = total
        f["mid_low"][...] = total.astype(jnp.bfloat16)
        second.append(
            to_peers(
                f["two"],
                lambda o: f["mid_low"].at[rows_at(peers[f["two"]][o] * f["piece"], f["piece"])]
                if f["split"]
                else f["mid_low"],
                lambda o: f["sums2"].at[o],
                s2_send.at[h],
                s2_recv.at[h],
            )
        )
    third = []
    for h, f in enumerate(flows):
        total = f["mid"][f["inner"]]
        for o, copy in enumerate(second[h], 1):
            copy.wait()
            total = total + f["sums2"][o].astype(jnp.float32)
        grad_ref[f["spot"], f["columns"]] = total.astype(jnp.bfloat16)
        if f["split"]:
            block_of = grad_ref.at[f["spot"], f["columns"]]
            third.append(
                to_peers(
                    f["two"],
                    lambda o: block_of,
                    lambda o: block_of,
                    s3_send.at[h],
                    s3_recv.at[h],
                )
            )
        else:
            third.append([])
    fourth = []
    for h, f in enumerate(flows):
        for copy in third[h]:
            copy.wait()
        rows_of = grad_ref.at[f["mine"], f["columns"]]
        fourth += to_peers(
            f["one"],
            lambda o: rows_of,
            lambda o: rows_of,
            s4_send.at[h],
            s4_recv.at[h],
        )
    for copy in fourth:
        copy.wait()


def body(
    feats,
    w_self,
    w_neigh,
    local_tiles,
    local_cols,
    cut_tiles,
    cut_src,
    send_block,
    send_live,
    cotangent,
):
    row_blocks, _, block, _ = local_tiles.shape
    features = feats.shape[1]
    n_dom, n_grp = lax.axis_size("dom"), lax.axis_size("grp")
    blocks = (row_blocks, block, features)
    halves = len(ORDERS)
    count = {"grp": n_grp, "dom": n_dom}
    most = max(n_grp, n_dom)
    sizes = []
    for one, two in ORDERS:
        rows = 2 * features // count[one]
        sizes.append((count[one], rows, count[two], piece_rows(rows, count[two])))
    width = features // halves
    dma = pltpu.SemaphoreType.DMA
    hbm = pl.BlockSpec(memory_space=pltpu.HBM)
    vmem = pl.BlockSpec(memory_space=pltpu.VMEM)
    out, grads = pl.pallas_call(
        functools.partial(kernel, n_dom, n_grp),
        out_shape=(
            jax.ShapeDtypeStruct(blocks, jnp.bfloat16),
            jax.ShapeDtypeStruct((2 * features, features), jnp.bfloat16),
        ),
        in_specs=[hbm] * 10,
        out_specs=(vmem, vmem),
        scratch_shapes=[
            pltpu.SMEM(local_cols.shape, jnp.int32),
            pltpu.SMEM(cut_src.shape, jnp.int32),
            pltpu.SMEM(send_block.shape, jnp.int32),
            pltpu.SMEM(send_live.shape, jnp.int32),
            pltpu.VMEM(w_self.shape, jnp.bfloat16),
            pltpu.VMEM(w_neigh.shape, jnp.bfloat16),
            pltpu.VMEM(local_tiles.shape, jnp.bfloat16),
            pltpu.VMEM(cut_tiles.shape, jnp.bfloat16),
            pltpu.VMEM(blocks, jnp.bfloat16),
            pltpu.VMEM(blocks, jnp.bfloat16),
            pltpu.VMEM((n_grp * row_blocks, block, features), jnp.bfloat16),
            pltpu.VMEM((n_dom, block, features), jnp.bfloat16),
            pltpu.VMEM((n_dom, block, features), jnp.bfloat16),
            pltpu.VMEM(blocks, jnp.float32),
            pltpu.VMEM(blocks, jnp.float32),
            pltpu.VMEM((halves, 2 * features, width), jnp.float32),
            pltpu.VMEM((halves, 2 * features, width), jnp.bfloat16),
        ]
        + [pltpu.VMEM((n, r, width), jnp.bfloat16) for n, r, _, _ in sizes]
        + [pltpu.VMEM((r, width), jnp.float32) for _, r, _, _ in sizes]
        + [pltpu.VMEM((r, width), jnp.bfloat16) for _, r, _, _ in sizes]
        + [pltpu.VMEM((n, p, width), jnp.bfloat16) for _, _, n, p in sizes]
        + [
            dma((11,)),
        ]
        + [dma((n_grp,))] * 2
        + [dma((n_dom,))] * 2
        + [dma((halves, most))] * 8,
        compiler_params=pltpu.CompilerParams(
            collective_id=0, has_side_effects=True, vmem_limit_bytes=60 * 2**20
        ),
    )(
        local_cols,
        cut_src,
        send_block,
        send_live,
        feats.reshape(blocks),
        w_self,
        w_neigh,
        local_tiles,
        cut_tiles,
        cotangent.reshape(blocks),
    )
    summed = grads.astype(jnp.float32)
    return (out.reshape(feats.shape), summed[:features], summed[features:])


def solution(mesh):
    return jax.shard_map(
        body,
        mesh=mesh,
        in_specs=(
            P(("dom", "grp"), None),
            P(),
            P(),
            P(("dom", "grp"), None, None, None),
            P(("dom", "grp"), None),
            P(("dom", "grp"), None, None, None),
            P(("dom", "grp"), None),
            P(("dom", "grp"), None),
            P(("dom", "grp"), None),
            P(("dom", "grp"), None),
        ),
        out_specs=(P(("dom", "grp"), None), P(), P()),
        check_vma=False,
    )
```

```python
import functools

import jax
import jax.numpy as jnp
from jax import lax
from jax.experimental import pallas as pl
from jax.experimental.pallas import tpu as pltpu
from jax.sharding import PartitionSpec as P

MESH = pl.DeviceIdType.MESH
PACK = 16
ORDERS = (("grp", "dom"), ("dom", "grp"))


def piece_rows(rows, n):
    return rows // n if rows % (PACK * n) == 0 else rows


def f32_dot(a, b):
    return jnp.dot(a, b, preferred_element_type=jnp.float32)


def kernel(
    n_dom,
    n_grp,
    cols_hbm,
    src_hbm,
    block_hbm,
    live_hbm,
    feats_hbm,
    w_self_hbm,
    w_neigh_hbm,
    local_hbm,
    cut_hbm,
    cot_hbm,
    out_ref,
    grad_ref,
    cols_ref,
    src_ref,
    block_ref,
    live_ref,
    w_self_ref,
    w_neigh_ref,
    local_ref,
    cut_ref,
    cot_ref,
    feats_ref,
    near,
    outgoing,
    far,
    acc,
    pre,
    part,
    part_low,
    sums1_a,
    sums1_b,
    mid_a,
    mid_b,
    low_a,
    low_b,
    sums2_a,
    sums2_b,
    load_sem,
    near_send,
    near_recv,
    far_send,
    far_recv,
    s1_send,
    s1_recv,
    s2_send,
    s2_recv,
    s3_send,
    s3_recv,
    s4_send,
    s4_recv,
):
    sums1, mid, mid_low = (sums1_a, sums1_b), (mid_a, mid_b), (low_a, low_b)
    sums2 = (sums2_a, sums2_b)
    row_blocks, local_slots, block, _ = local_ref.shape
    cut_slots = cut_ref.shape[1]
    features = w_self_ref.shape[0]
    width = part.shape[2]
    me_d, me_g = lax.axis_index("dom"), lax.axis_index("grp")
    dom_peer = [lax.rem(me_d + o, n_dom) for o in range(n_dom)]
    grp_peer = [lax.rem(me_g + o, n_grp) for o in range(n_grp)]

    def remote(src, dst, send, recv, o, axis):
        peer = dom_peer[o] if axis == "dom" else grp_peer[o]
        return pltpu.make_async_remote_copy(
            src_ref=src,
            dst_ref=dst,
            send_sem=send,
            recv_sem=recv,
            device_id={axis: peer},
            device_id_type=MESH,
        )

    def begin(copies):
        for copy in copies:
            copy.start()
        return copies

    loads = begin(
        [
            pltpu.make_async_copy(src, dst, load_sem.at[i])
            for i, (src, dst) in enumerate(
                (
                    (block_hbm, block_ref),
                    (live_hbm, live_ref),
                    (feats_hbm, feats_ref),
                    (feats_hbm, near.at[pl.ds(0, row_blocks)]),
                    (cols_hbm, cols_ref),
                    (src_hbm, src_ref),
                    (w_self_hbm, w_self_ref),
                    (local_hbm, local_ref),
                    (cut_hbm, cut_ref),
                    (w_neigh_hbm, w_neigh_ref),
                    (cot_hbm, cot_ref),
                )
            )
        ]
    )
    barrier = pltpu.get_barrier_semaphore()
    for o in range(1, n_dom):
        pl.semaphore_signal(barrier, inc=1, device_id={"dom": dom_peer[o]}, device_id_type=MESH)
    for o in range(1, n_grp):
        pl.semaphore_signal(barrier, inc=1, device_id={"grp": grp_peer[o]}, device_id_type=MESH)
    for load in loads[:3]:
        load.wait()

    for o in range(n_dom):
        alive = live_ref[0, dom_peer[o]].astype(jnp.float32)
        chosen = feats_ref[block_ref[0, dom_peer[o]]].astype(jnp.float32)
        target = far if o == 0 else outgoing
        target[o] = (chosen * alive).astype(jnp.bfloat16)
    pl.semaphore_wait(barrier, n_dom + n_grp - 2)

    far_copies = begin(
        [
            remote(outgoing.at[o], far.at[o], far_send.at[o], far_recv.at[o], o, "dom")
            for o in range(1, n_dom)
        ]
    )
    near_copies = begin(
        [
            remote(
                feats_ref,
                near.at[pl.ds(o * row_blocks, row_blocks)],
                near_send.at[o],
                near_recv.at[o],
                o,
                "grp",
            )
            for o in range(1, n_grp)
        ]
    )

    for load in loads[3:]:
        load.wait()
    for b in range(row_blocks):
        pre[b] = f32_dot(feats_ref[b], w_self_ref[...])
    for copy in near_copies:
        copy.wait_recv()
    for b in range(row_blocks):
        total = jnp.zeros((block, features), jnp.float32)
        for k in range(local_slots):
            col = cols_ref[b, k]
            owner = lax.div(col, row_blocks)
            slot = lax.rem(me_g - owner + n_grp, n_grp)
            where = slot * row_blocks + lax.rem(col, row_blocks)
            total = total + f32_dot(local_ref[b, k], near[where])
        acc[b] = total

    for copy in far_copies:
        copy.wait_recv()
    grads_own = jnp.zeros((features, features), jnp.float32)
    grads_agg = jnp.zeros((features, features), jnp.float32)
    for b in range(row_blocks):
        total = acc[b]
        for k in range(cut_slots):
            slot = lax.rem(n_dom - src_ref[b, k], n_dom)
            total = total + f32_dot(cut_ref[b, k], far[slot])
        agg = total.astype(jnp.bfloat16)
        own = feats_ref[b]
        preact = pre[b] + f32_dot(agg, w_neigh_ref[...])
        sig = jax.nn.sigmoid(preact)
        out_ref[b] = (preact * sig).astype(jnp.bfloat16)
        grad_pre = (
            cot_ref[b].astype(jnp.float32) * sig * (1.0 + preact * (1.0 - sig))
        ).astype(jnp.bfloat16)
        dims = (((0,), (0,)), ((), ()))
        grads_own = grads_own + lax.dot_general(
            own, grad_pre, dims, preferred_element_type=jnp.float32
        )
        grads_agg = grads_agg + lax.dot_general(
            agg, grad_pre, dims, preferred_element_type=jnp.float32
        )

    peers = {"grp": grp_peer, "dom": dom_peer}
    here = {"grp": me_g, "dom": me_d}
    count = {"grp": n_grp, "dom": n_dom}

    def rows_at(start, size):
        return pl.ds(pl.multiple_of(start, size), size)

    def to_peers(axis, src, dst, send, recv):
        return begin(
            [
                remote(src(o), dst(o), send.at[o], recv.at[o], o, axis)
                for o in range(1, count[axis])
            ]
        )

    flows = []
    for h, (one, two) in enumerate(ORDERS):
        rows = 2 * features // count[one]
        piece = piece_rows(rows, count[two])
        split = piece < rows
        flows.append(
            dict(
                one=one,
                two=two,
                rows=rows,
                piece=piece,
                split=split,
                columns=pl.ds(h * width, width),
                mine=rows_at(here[one] * rows, rows),
                inner=rows_at(here[two] * piece, piece) if split else pl.ds(0, rows),
                spot=rows_at(here[one] * rows + (here[two] * piece if split else 0), piece),
                sums1=sums1[h],
                mid=mid[h],
                mid_low=mid_low[h],
                sums2=sums2[h],
            )
        )

    first = []
    for h, f in enumerate(flows):
        cut = slice(h * width, (h + 1) * width)
        part[h, 0:features] = grads_own[:, cut]
        part[h, features : 2 * features] = grads_agg[:, cut]
        part_low[h, 0:features] = grads_own[:, cut].astype(jnp.bfloat16)
        part_low[h, features : 2 * features] = grads_agg[:, cut].astype(jnp.bfloat16)
        first.append(
            to_peers(
                f["one"],
                lambda o: part_low.at[h, rows_at(peers[f["one"]][o] * f["rows"], f["rows"])],
                lambda o: f["sums1"].at[o],
                s1_send.at[h],
                s1_recv.at[h],
            )
        )
    second = []
    for h, f in enumerate(flows):
        total = part[h, f["mine"]]
        for o, copy in enumerate(first[h], 1):
            copy.wait_recv()
            total = total + f["sums1"][o].astype(jnp.float32)
        f["mid"][...] = total
        f["mid_low"][...] = total.astype(jnp.bfloat16)
        second.append(
            to_peers(
                f["two"],
                lambda o: f["mid_low"].at[rows_at(peers[f["two"]][o] * f["piece"], f["piece"])]
                if f["split"]
                else f["mid_low"],
                lambda o: f["sums2"].at[o],
                s2_send.at[h],
                s2_recv.at[h],
            )
        )
    third = []
    for h, f in enumerate(flows):
        total = f["mid"][f["inner"]]
        for o, copy in enumerate(second[h], 1):
            copy.wait_recv()
            total = total + f["sums2"][o].astype(jnp.float32)
        grad_ref[f["spot"], f["columns"]] = total.astype(jnp.bfloat16)
        if f["split"]:
            block_of = grad_ref.at[f["spot"], f["columns"]]
            third.append(
                to_peers(
                    f["two"],
                    lambda o: block_of,
                    lambda o: block_of,
                    s3_send.at[h],
                    s3_recv.at[h],
                )
            )
        else:
            third.append([])
    fourth = []
    for h, f in enumerate(flows):
        for copy in third[h]:
            copy.wait_recv()
        rows_of = grad_ref.at[f["mine"], f["columns"]]
        fourth += to_peers(
            f["one"],
            lambda o: rows_of,
            lambda o: rows_of,
            s4_send.at[h],
            s4_recv.at[h],
        )
    for copy in fourth:
        copy.wait_recv()

    sent = [far_copies, near_copies, *first, *second, *third, fourth]
    for copy in [copy for group in sent for copy in group]:
        copy.wait_send()


def body(
    feats,
    w_self,
    w_neigh,
    local_tiles,
    local_cols,
    cut_tiles,
    cut_src,
    send_block,
    send_live,
    cotangent,
):
    row_blocks, _, block, _ = local_tiles.shape
    features = feats.shape[1]
    n_dom, n_grp = lax.axis_size("dom"), lax.axis_size("grp")
    blocks = (row_blocks, block, features)
    halves = len(ORDERS)
    count = {"grp": n_grp, "dom": n_dom}
    most = max(n_grp, n_dom)
    sizes = []
    for one, two in ORDERS:
        rows = 2 * features // count[one]
        sizes.append((count[one], rows, count[two], piece_rows(rows, count[two])))
    width = features // halves
    dma = pltpu.SemaphoreType.DMA
    hbm = pl.BlockSpec(memory_space=pltpu.HBM)
    vmem = pl.BlockSpec(memory_space=pltpu.VMEM)
    out, grads = pl.pallas_call(
        functools.partial(kernel, n_dom, n_grp),
        out_shape=(
            jax.ShapeDtypeStruct(blocks, jnp.bfloat16),
            jax.ShapeDtypeStruct((2 * features, features), jnp.bfloat16),
        ),
        in_specs=[hbm] * 10,
        out_specs=(vmem, vmem),
        scratch_shapes=[
            pltpu.SMEM(local_cols.shape, jnp.int32),
            pltpu.SMEM(cut_src.shape, jnp.int32),
            pltpu.SMEM(send_block.shape, jnp.int32),
            pltpu.SMEM(send_live.shape, jnp.int32),
            pltpu.VMEM(w_self.shape, jnp.bfloat16),
            pltpu.VMEM(w_neigh.shape, jnp.bfloat16),
            pltpu.VMEM(local_tiles.shape, jnp.bfloat16),
            pltpu.VMEM(cut_tiles.shape, jnp.bfloat16),
            pltpu.VMEM(blocks, jnp.bfloat16),
            pltpu.VMEM(blocks, jnp.bfloat16),
            pltpu.VMEM((n_grp * row_blocks, block, features), jnp.bfloat16),
            pltpu.VMEM((n_dom, block, features), jnp.bfloat16),
            pltpu.VMEM((n_dom, block, features), jnp.bfloat16),
            pltpu.VMEM(blocks, jnp.float32),
            pltpu.VMEM(blocks, jnp.float32),
            pltpu.VMEM((halves, 2 * features, width), jnp.float32),
            pltpu.VMEM((halves, 2 * features, width), jnp.bfloat16),
        ]
        + [pltpu.VMEM((n, r, width), jnp.bfloat16) for n, r, _, _ in sizes]
        + [pltpu.VMEM((r, width), jnp.float32) for _, r, _, _ in sizes]
        + [pltpu.VMEM((r, width), jnp.bfloat16) for _, r, _, _ in sizes]
        + [pltpu.VMEM((n, p, width), jnp.bfloat16) for _, _, n, p in sizes]
        + [
            dma((11,)),
        ]
        + [dma((n_grp,))] * 2
        + [dma((n_dom,))] * 2
        + [dma((halves, most))] * 8,
        compiler_params=pltpu.CompilerParams(
            collective_id=0, has_side_effects=True, vmem_limit_bytes=32 * 2**20
        ),
    )(
        *(
            pltpu.with_memory_space_constraint(x, pltpu.HBM)
            for x in (
                local_cols,
                cut_src,
                send_block,
                send_live,
                feats.reshape(blocks),
                w_self,
                w_neigh,
                local_tiles,
                cut_tiles,
                cotangent.reshape(blocks),
            )
        )
    )
    summed = grads.astype(jnp.float32)
    return (out.reshape(feats.shape), summed[:features], summed[features:])


def solution(mesh):
    return jax.shard_map(
        body,
        mesh=mesh,
        in_specs=(
            P(("dom", "grp"), None),
            P(),
            P(),
            P(("dom", "grp"), None, None, None),
            P(("dom", "grp"), None),
            P(("dom", "grp"), None, None, None),
            P(("dom", "grp"), None),
            P(("dom", "grp"), None),
            P(("dom", "grp"), None),
            P(("dom", "grp"), None),
        ),
        out_specs=(P(("dom", "grp"), None), P(), P()),
        check_vma=False,
    )
```

```python
import functools

import jax
import jax.numpy as jnp
from jax import lax
from jax.experimental import pallas as pl
from jax.experimental.pallas import tpu as pltpu
from jax.sharding import PartitionSpec as P

MESH = pl.DeviceIdType.MESH
PACK = 16
FEW = 4
ORDERS = (("grp", "dom"), ("dom", "grp"))


def piece_rows(rows, n):
    return rows // n if n > FEW and rows % (PACK * n) == 0 else rows


def f32_dot(a, b):
    return jnp.dot(a, b, preferred_element_type=jnp.float32)


def kernel(
    n_dom,
    n_grp,
    cols_hbm,
    src_hbm,
    block_hbm,
    live_hbm,
    feats_hbm,
    w_self_hbm,
    w_neigh_hbm,
    local_hbm,
    cut_hbm,
    cot_hbm,
    out_ref,
    grad_ref,
    cols_ref,
    src_ref,
    block_ref,
    live_ref,
    w_self_ref,
    w_neigh_ref,
    local_ref,
    cut_ref,
    cot_ref,
    feats_ref,
    near,
    outgoing,
    far,
    acc,
    pre,
    part,
    part_low,
    sums1_a,
    sums1_b,
    mid_a,
    mid_b,
    low_a,
    low_b,
    sums2_a,
    sums2_b,
    load_sem,
    near_send,
    near_recv,
    far_send,
    far_recv,
    s1_send,
    s1_recv,
    s2_send,
    s2_recv,
    s3_send,
    s3_recv,
    s4_send,
    s4_recv,
):
    sums1, mid, mid_low = (sums1_a, sums1_b), (mid_a, mid_b), (low_a, low_b)
    sums2 = (sums2_a, sums2_b)
    row_blocks, local_slots, block, _ = local_ref.shape
    cut_slots = cut_ref.shape[1]
    features = w_self_ref.shape[0]
    width = part.shape[2]
    me_d, me_g = lax.axis_index("dom"), lax.axis_index("grp")
    dom_peer = [lax.rem(me_d + o, n_dom) for o in range(n_dom)]
    grp_peer = [lax.rem(me_g + o, n_grp) for o in range(n_grp)]

    def remote(src, dst, send, recv, o, axis):
        peer = dom_peer[o] if axis == "dom" else grp_peer[o]
        return pltpu.make_async_remote_copy(
            src_ref=src,
            dst_ref=dst,
            send_sem=send,
            recv_sem=recv,
            device_id={axis: peer},
            device_id_type=MESH,
        )

    def begin(copies):
        for copy in copies:
            copy.start()
        return copies

    barrier = pltpu.get_barrier_semaphore()
    for o in range(1, n_dom):
        pl.semaphore_signal(barrier, inc=1, device_id={"dom": dom_peer[o]}, device_id_type=MESH)
    for o in range(1, n_grp):
        pl.semaphore_signal(barrier, inc=1, device_id={"grp": grp_peer[o]}, device_id_type=MESH)
    loads = begin(
        [
            pltpu.make_async_copy(src, dst, load_sem.at[i])
            for i, (src, dst) in enumerate(
                (
                    (block_hbm, block_ref),
                    (live_hbm, live_ref),
                    (feats_hbm, feats_ref),
                    (feats_hbm, near.at[pl.ds(0, row_blocks)]),
                    (cols_hbm, cols_ref),
                    (src_hbm, src_ref),
                    (w_self_hbm, w_self_ref),
                    (local_hbm, local_ref),
                    (cut_hbm, cut_ref),
                    (w_neigh_hbm, w_neigh_ref),
                    (cot_hbm, cot_ref),
                )
            )
        ]
    )
    for load in loads[:3]:
        load.wait()

    for o in range(n_dom):
        alive = live_ref[0, dom_peer[o]].astype(jnp.float32)
        chosen = feats_ref[block_ref[0, dom_peer[o]]].astype(jnp.float32)
        target = far if o == 0 else outgoing
        target[o] = (chosen * alive).astype(jnp.bfloat16)
    pl.semaphore_wait(barrier, n_dom + n_grp - 2)

    far_copies = begin(
        [
            remote(outgoing.at[o], far.at[o], far_send.at[o], far_recv.at[o], o, "dom")
            for o in range(1, n_dom)
        ]
    )
    near_copies = begin(
        [
            remote(
                feats_ref,
                near.at[pl.ds(o * row_blocks, row_blocks)],
                near_send.at[o],
                near_recv.at[o],
                o,
                "grp",
            )
            for o in range(1, n_grp)
        ]
    )

    for load in loads[3:]:
        load.wait()
    for b in range(row_blocks):
        pre[b] = f32_dot(feats_ref[b], w_self_ref[...])
    for copy in near_copies:
        copy.wait_recv()
    for b in range(row_blocks):
        total = jnp.zeros((block, features), jnp.float32)
        for k in range(local_slots):
            col = cols_ref[b, k]
            owner = lax.div(col, row_blocks)
            slot = lax.rem(me_g - owner + n_grp, n_grp)
            where = slot * row_blocks + lax.rem(col, row_blocks)
            total = total + f32_dot(local_ref[b, k], near[where])
        acc[b] = total

    for copy in far_copies:
        copy.wait_recv()
    grads_own = jnp.zeros((features, features), jnp.float32)
    grads_agg = jnp.zeros((features, features), jnp.float32)
    for b in range(row_blocks):
        total = acc[b]
        for k in range(cut_slots):
            slot = lax.rem(n_dom - src_ref[b, k], n_dom)
            total = total + f32_dot(cut_ref[b, k], far[slot])
        agg = total.astype(jnp.bfloat16)
        own = feats_ref[b]
        preact = pre[b] + f32_dot(agg, w_neigh_ref[...])
        sig = jax.nn.sigmoid(preact)
        out_ref[b] = (preact * sig).astype(jnp.bfloat16)
        grad_pre = (
            cot_ref[b].astype(jnp.float32) * sig * (1.0 + preact * (1.0 - sig))
        ).astype(jnp.bfloat16)
        dims = (((0,), (0,)), ((), ()))
        grads_own = grads_own + lax.dot_general(
            own, grad_pre, dims, preferred_element_type=jnp.float32
        )
        grads_agg = grads_agg + lax.dot_general(
            agg, grad_pre, dims, preferred_element_type=jnp.float32
        )

    peers = {"grp": grp_peer, "dom": dom_peer}
    here = {"grp": me_g, "dom": me_d}
    count = {"grp": n_grp, "dom": n_dom}

    def rows_at(start, size):
        return pl.ds(pl.multiple_of(start, size), size)

    def to_peers(axis, src, dst, send, recv):
        return begin(
            [
                remote(src(o), dst(o), send.at[o], recv.at[o], o, axis)
                for o in range(1, count[axis])
            ]
        )

    flows = []
    for h, (one, two) in enumerate(ORDERS):
        rows = 2 * features // count[one]
        piece = piece_rows(rows, count[two])
        split = piece < rows
        flows.append(
            dict(
                one=one,
                two=two,
                rows=rows,
                piece=piece,
                split=split,
                columns=pl.ds(h * width, width),
                mine=rows_at(here[one] * rows, rows),
                inner=rows_at(here[two] * piece, piece) if split else pl.ds(0, rows),
                spot=rows_at(here[one] * rows + (here[two] * piece if split else 0), piece),
                sums1=sums1[h],
                mid=mid[h],
                mid_low=mid_low[h],
                sums2=sums2[h],
            )
        )

    first = []
    for h, f in enumerate(flows):
        cut = slice(h * width, (h + 1) * width)
        part[h, 0:features] = grads_own[:, cut]
        part[h, features : 2 * features] = grads_agg[:, cut]
        part_low[h, 0:features] = grads_own[:, cut].astype(jnp.bfloat16)
        part_low[h, features : 2 * features] = grads_agg[:, cut].astype(jnp.bfloat16)
        first.append(
            to_peers(
                f["one"],
                lambda o: part_low.at[h, rows_at(peers[f["one"]][o] * f["rows"], f["rows"])],
                lambda o: f["sums1"].at[o],
                s1_send.at[h],
                s1_recv.at[h],
            )
        )
    second = []
    for h, f in enumerate(flows):
        total = part[h, f["mine"]]
        for o, copy in enumerate(first[h], 1):
            copy.wait_recv()
            total = total + f["sums1"][o].astype(jnp.float32)
        f["mid"][...] = total
        f["mid_low"][...] = total.astype(jnp.bfloat16)
        second.append(
            to_peers(
                f["two"],
                lambda o: f["mid_low"].at[rows_at(peers[f["two"]][o] * f["piece"], f["piece"])]
                if f["split"]
                else f["mid_low"],
                lambda o: f["sums2"].at[o if f["split"] else here[f["two"]]],
                s2_send.at[h],
                s2_recv.at[h],
            )
        )
    third, fourth = [], []

    def gather(h, f):
        rows_of = grad_ref.at[f["mine"], f["columns"]]
        return to_peers(
            f["one"], lambda o: rows_of, lambda o: rows_of, s4_send.at[h], s4_recv.at[h]
        )

    for h, f in enumerate(flows):
        if f["split"]:
            total = f["mid"][f["inner"]]
            for o, copy in enumerate(second[h], 1):
                copy.wait_recv()
                total = total + f["sums2"][o].astype(jnp.float32)
        else:
            f["sums2"][here[f["two"]]] = f["mid_low"][...]
            for copy in second[h]:
                copy.wait_recv()
            total = f["sums2"][0].astype(jnp.float32)
            for o in range(1, count[f["two"]]):
                total = total + f["sums2"][o].astype(jnp.float32)
        grad_ref[f["spot"], f["columns"]] = total.astype(jnp.bfloat16)
        if f["split"]:
            block_of = grad_ref.at[f["spot"], f["columns"]]
            third.append(
                to_peers(
                    f["two"],
                    lambda o: block_of,
                    lambda o: block_of,
                    s3_send.at[h],
                    s3_recv.at[h],
                )
            )
        else:
            third.append([])
            fourth += gather(h, f)
    for h, f in enumerate(flows):
        if f["split"]:
            for copy in third[h]:
                copy.wait_recv()
            fourth += gather(h, f)
    for copy in fourth:
        copy.wait_recv()

    sent = [far_copies, near_copies, *first, *second, *third, fourth]
    for copy in [copy for group in sent for copy in group]:
        copy.wait_send()


def body(
    feats,
    w_self,
    w_neigh,
    local_tiles,
    local_cols,
    cut_tiles,
    cut_src,
    send_block,
    send_live,
    cotangent,
):
    row_blocks, _, block, _ = local_tiles.shape
    features = feats.shape[1]
    n_dom, n_grp = lax.axis_size("dom"), lax.axis_size("grp")
    blocks = (row_blocks, block, features)
    halves = len(ORDERS)
    count = {"grp": n_grp, "dom": n_dom}
    most = max(n_grp, n_dom)
    sizes = []
    for one, two in ORDERS:
        rows = 2 * features // count[one]
        sizes.append((count[one], rows, count[two], piece_rows(rows, count[two])))
    width = features // halves
    dma = pltpu.SemaphoreType.DMA
    hbm = pl.BlockSpec(memory_space=pltpu.HBM)
    vmem = pl.BlockSpec(memory_space=pltpu.VMEM)
    out, grads = pl.pallas_call(
        functools.partial(kernel, n_dom, n_grp),
        out_shape=(
            jax.ShapeDtypeStruct(blocks, jnp.bfloat16),
            jax.ShapeDtypeStruct((2 * features, features), jnp.bfloat16),
        ),
        in_specs=[hbm] * 10,
        out_specs=(vmem, vmem),
        scratch_shapes=[
            pltpu.SMEM(local_cols.shape, jnp.int32),
            pltpu.SMEM(cut_src.shape, jnp.int32),
            pltpu.SMEM(send_block.shape, jnp.int32),
            pltpu.SMEM(send_live.shape, jnp.int32),
            pltpu.VMEM(w_self.shape, jnp.bfloat16),
            pltpu.VMEM(w_neigh.shape, jnp.bfloat16),
            pltpu.VMEM(local_tiles.shape, jnp.bfloat16),
            pltpu.VMEM(cut_tiles.shape, jnp.bfloat16),
            pltpu.VMEM(blocks, jnp.bfloat16),
            pltpu.VMEM(blocks, jnp.bfloat16),
            pltpu.VMEM((n_grp * row_blocks, block, features), jnp.bfloat16),
            pltpu.VMEM((n_dom, block, features), jnp.bfloat16),
            pltpu.VMEM((n_dom, block, features), jnp.bfloat16),
            pltpu.VMEM(blocks, jnp.float32),
            pltpu.VMEM(blocks, jnp.float32),
            pltpu.VMEM((halves, 2 * features, width), jnp.float32),
            pltpu.VMEM((halves, 2 * features, width), jnp.bfloat16),
        ]
        + [pltpu.VMEM((n, r, width), jnp.bfloat16) for n, r, _, _ in sizes]
        + [pltpu.VMEM((r, width), jnp.float32) for _, r, _, _ in sizes]
        + [pltpu.VMEM((r, width), jnp.bfloat16) for _, r, _, _ in sizes]
        + [pltpu.VMEM((n, p, width), jnp.bfloat16) for _, _, n, p in sizes]
        + [
            dma((11,)),
        ]
        + [dma((n_grp,))] * 2
        + [dma((n_dom,))] * 2
        + [dma((halves, most))] * 8,
        compiler_params=pltpu.CompilerParams(
            collective_id=0, has_side_effects=True, vmem_limit_bytes=32 * 2**20
        ),
    )(
        *(
            pltpu.with_memory_space_constraint(x, pltpu.HBM)
            for x in (
                local_cols,
                cut_src,
                send_block,
                send_live,
                feats.reshape(blocks),
                w_self,
                w_neigh,
                local_tiles,
                cut_tiles,
                cotangent.reshape(blocks),
            )
        )
    )
    summed = grads.astype(jnp.float32)
    return (out.reshape(feats.shape), summed[:features], summed[features:])


def solution(mesh):
    return jax.shard_map(
        body,
        mesh=mesh,
        in_specs=(
            P(("dom", "grp"), None),
            P(),
            P(),
            P(("dom", "grp"), None, None, None),
            P(("dom", "grp"), None),
            P(("dom", "grp"), None, None, None),
            P(("dom", "grp"), None),
            P(("dom", "grp"), None),
            P(("dom", "grp"), None),
            P(("dom", "grp"), None),
        ),
        out_specs=(P(("dom", "grp"), None), P(), P()),
        check_vma=False,
    )
```

```python
import functools

import jax
import jax.numpy as jnp
from jax import lax
from jax.experimental import pallas as pl
from jax.experimental.pallas import tpu as pltpu
from jax.sharding import PartitionSpec as P

MESH = pl.DeviceIdType.MESH
PACK = 16
FEW = 4
ORDERS = (("grp", "dom"), ("dom", "grp"))


def piece_rows(rows, n):
    return rows // n if n > FEW and rows % (PACK * n) == 0 else rows


def f32_dot(a, b):
    return jnp.dot(a, b, preferred_element_type=jnp.float32)


def kernel(
    n_dom,
    n_grp,
    cols_hbm,
    src_hbm,
    block_hbm,
    live_hbm,
    feats_hbm,
    w_self_hbm,
    w_neigh_hbm,
    local_hbm,
    cut_hbm,
    cot_hbm,
    out_ref,
    grad_ref,
    cols_ref,
    src_ref,
    block_ref,
    live_ref,
    w_self_ref,
    w_neigh_ref,
    local_ref,
    cut_ref,
    cot_ref,
    feats_ref,
    near,
    outgoing,
    far,
    acc,
    pre,
    part,
    part_low,
    sums1_a,
    sums1_b,
    mid_a,
    mid_b,
    low_a,
    low_b,
    sums2_a,
    sums2_b,
    load_sem,
    near_send,
    near_recv,
    far_send,
    far_recv,
    s1_send,
    s1_recv,
    s2_send,
    s2_recv,
    s3_send,
    s3_recv,
    s4_send,
    s4_recv,
):
    sums1, mid, mid_low = (sums1_a, sums1_b), (mid_a, mid_b), (low_a, low_b)
    sums2 = (sums2_a, sums2_b)
    row_blocks, local_slots, block, _ = local_ref.shape
    cut_slots = cut_ref.shape[1]
    features = w_self_ref.shape[0]
    width = part.shape[2]
    me_d, me_g = lax.axis_index("dom"), lax.axis_index("grp")
    dom_peer = [lax.rem(me_d + o, n_dom) for o in range(n_dom)]
    grp_peer = [lax.rem(me_g + o, n_grp) for o in range(n_grp)]

    def remote(src, dst, send, recv, o, axis):
        peer = dom_peer[o] if axis == "dom" else grp_peer[o]
        return pltpu.make_async_remote_copy(
            src_ref=src,
            dst_ref=dst,
            send_sem=send,
            recv_sem=recv,
            device_id={axis: peer},
            device_id_type=MESH,
        )

    def begin(copies):
        for copy in copies:
            copy.start()
        return copies

    barrier = pltpu.get_barrier_semaphore()
    for o in range(1, n_dom):
        pl.semaphore_signal(barrier, inc=1, device_id={"dom": dom_peer[o]}, device_id_type=MESH)
    for o in range(1, n_grp):
        pl.semaphore_signal(barrier, inc=1, device_id={"grp": grp_peer[o]}, device_id_type=MESH)
    loads = begin(
        [
            pltpu.make_async_copy(src, dst, load_sem.at[i])
            for i, (src, dst) in enumerate(
                (
                    (block_hbm, block_ref),
                    (live_hbm, live_ref),
                    (feats_hbm, feats_ref),
                    (feats_hbm, near.at[pl.ds(0, row_blocks)]),
                    (cols_hbm, cols_ref),
                    (src_hbm, src_ref),
                    (w_self_hbm, w_self_ref),
                    (local_hbm, local_ref),
                    (cut_hbm, cut_ref),
                    (w_neigh_hbm, w_neigh_ref),
                    (cot_hbm, cot_ref),
                )
            )
        ]
    )
    for load in loads[:3]:
        load.wait()

    for o in range(n_dom):
        alive = live_ref[0, dom_peer[o]].astype(jnp.float32)
        chosen = feats_ref[block_ref[0, dom_peer[o]]].astype(jnp.float32)
        target = far if o == 0 else outgoing
        target[o] = (chosen * alive).astype(jnp.bfloat16)
    pl.semaphore_wait(barrier, n_dom + n_grp - 2)

    far_copies = begin(
        [
            remote(outgoing.at[o], far.at[o], far_send.at[o], far_recv.at[o], o, "dom")
            for o in sorted(range(1, n_dom), key=lambda o: abs(2 * o - n_dom))
        ]
    )
    near_copies = begin(
        [
            remote(
                feats_ref,
                near.at[pl.ds(o * row_blocks, row_blocks)],
                near_send.at[o],
                near_recv.at[o],
                o,
                "grp",
            )
            for o in range(1, n_grp)
        ]
    )

    for load in loads[3:]:
        load.wait()
    for b in range(row_blocks):
        pre[b] = f32_dot(feats_ref[b], w_self_ref[...])
    for copy in near_copies:
        copy.wait_recv()
    for b in range(row_blocks):
        total = jnp.zeros((block, features), jnp.float32)
        for k in range(local_slots):
            col = cols_ref[b, k]
            owner = lax.div(col, row_blocks)
            slot = lax.rem(me_g - owner + n_grp, n_grp)
            where = slot * row_blocks + lax.rem(col, row_blocks)
            total = total + f32_dot(local_ref[b, k], near[where])
        acc[b] = total

    for copy in far_copies:
        copy.wait_recv()
    grads_own = jnp.zeros((features, features), jnp.float32)
    grads_agg = jnp.zeros((features, features), jnp.float32)
    for b in range(row_blocks):
        total = acc[b]
        for k in range(cut_slots):
            slot = lax.rem(n_dom - src_ref[b, k], n_dom)
            total = total + f32_dot(cut_ref[b, k], far[slot])
        agg = total.astype(jnp.bfloat16)
        own = feats_ref[b]
        preact = pre[b] + f32_dot(agg, w_neigh_ref[...])
        sig = jax.nn.sigmoid(preact)
        out_ref[b] = (preact * sig).astype(jnp.bfloat16)
        grad_pre = (
            cot_ref[b].astype(jnp.float32) * sig * (1.0 + preact * (1.0 - sig))
        ).astype(jnp.bfloat16)
        dims = (((0,), (0,)), ((), ()))
        grads_own = grads_own + lax.dot_general(
            own, grad_pre, dims, preferred_element_type=jnp.float32
        )
        grads_agg = grads_agg + lax.dot_general(
            agg, grad_pre, dims, preferred_element_type=jnp.float32
        )

    peers = {"grp": grp_peer, "dom": dom_peer}
    here = {"grp": me_g, "dom": me_d}
    count = {"grp": n_grp, "dom": n_dom}

    def rows_at(start, size):
        return pl.ds(pl.multiple_of(start, size), size)

    def to_peers(axis, src, dst, send, recv):
        return begin(
            [
                remote(src(o), dst(o), send.at[o], recv.at[o], o, axis)
                for o in range(1, count[axis])
            ]
        )

    flows = []
    for h, (one, two) in enumerate(ORDERS):
        rows = 2 * features // count[one]
        piece = piece_rows(rows, count[two])
        split = piece < rows
        flows.append(
            dict(
                one=one,
                two=two,
                rows=rows,
                piece=piece,
                split=split,
                columns=pl.ds(h * width, width),
                mine=rows_at(here[one] * rows, rows),
                inner=rows_at(here[two] * piece, piece) if split else pl.ds(0, rows),
                spot=rows_at(here[one] * rows + (here[two] * piece if split else 0), piece),
                sums1=sums1[h],
                mid=mid[h],
                mid_low=mid_low[h],
                sums2=sums2[h],
            )
        )

    first = []
    for h, f in enumerate(flows):
        cut = slice(h * width, (h + 1) * width)
        part[h, 0:features] = grads_own[:, cut]
        part[h, features : 2 * features] = grads_agg[:, cut]
        part_low[h, 0:features] = grads_own[:, cut].astype(jnp.bfloat16)
        part_low[h, features : 2 * features] = grads_agg[:, cut].astype(jnp.bfloat16)
        first.append(
            to_peers(
                f["one"],
                lambda o: part_low.at[h, rows_at(peers[f["one"]][o] * f["rows"], f["rows"])],
                lambda o: f["sums1"].at[o],
                s1_send.at[h],
                s1_recv.at[h],
            )
        )
    second = []
    for h, f in enumerate(flows):
        total = part[h, f["mine"]]
        for o, copy in enumerate(first[h], 1):
            copy.wait_recv()
            total = total + f["sums1"][o].astype(jnp.float32)
        f["mid"][...] = total
        f["mid_low"][...] = total.astype(jnp.bfloat16)
        second.append(
            to_peers(
                f["two"],
                lambda o: f["mid_low"].at[rows_at(peers[f["two"]][o] * f["piece"], f["piece"])]
                if f["split"]
                else f["mid_low"],
                lambda o: f["sums2"].at[o if f["split"] else here[f["two"]]],
                s2_send.at[h],
                s2_recv.at[h],
            )
        )
    third, fourth = [], []

    def gather(h, f):
        rows_of = grad_ref.at[f["mine"], f["columns"]]
        return to_peers(
            f["one"], lambda o: rows_of, lambda o: rows_of, s4_send.at[h], s4_recv.at[h]
        )

    for h, f in enumerate(flows):
        if f["split"]:
            total = f["mid"][f["inner"]]
            for o, copy in enumerate(second[h], 1):
                copy.wait_recv()
                total = total + f["sums2"][o].astype(jnp.float32)
        else:
            f["sums2"][here[f["two"]]] = f["mid_low"][...]
            for copy in second[h]:
                copy.wait_recv()
            total = f["sums2"][0].astype(jnp.float32)
            for o in range(1, count[f["two"]]):
                total = total + f["sums2"][o].astype(jnp.float32)
        grad_ref[f["spot"], f["columns"]] = total.astype(jnp.bfloat16)
        if f["split"]:
            block_of = grad_ref.at[f["spot"], f["columns"]]
            third.append(
                to_peers(
                    f["two"],
                    lambda o: block_of,
                    lambda o: block_of,
                    s3_send.at[h],
                    s3_recv.at[h],
                )
            )
        else:
            third.append([])
            fourth += gather(h, f)
    for h, f in enumerate(flows):
        if f["split"]:
            for copy in third[h]:
                copy.wait_recv()
            fourth += gather(h, f)
    for copy in fourth:
        copy.wait_recv()

    sent = [far_copies, near_copies, *first, *second, *third, fourth]
    for copy in [copy for group in sent for copy in group]:
        copy.wait_send()


def body(
    feats,
    w_self,
    w_neigh,
    local_tiles,
    local_cols,
    cut_tiles,
    cut_src,
    send_block,
    send_live,
    cotangent,
):
    row_blocks, _, block, _ = local_tiles.shape
    features = feats.shape[1]
    n_dom, n_grp = lax.axis_size("dom"), lax.axis_size("grp")
    blocks = (row_blocks, block, features)
    halves = len(ORDERS)
    count = {"grp": n_grp, "dom": n_dom}
    most = max(n_grp, n_dom)
    sizes = []
    for one, two in ORDERS:
        rows = 2 * features // count[one]
        sizes.append((count[one], rows, count[two], piece_rows(rows, count[two])))
    width = features // halves
    dma = pltpu.SemaphoreType.DMA
    hbm = pl.BlockSpec(memory_space=pltpu.HBM)
    vmem = pl.BlockSpec(memory_space=pltpu.VMEM)
    out, grads = pl.pallas_call(
        functools.partial(kernel, n_dom, n_grp),
        out_shape=(
            jax.ShapeDtypeStruct(blocks, jnp.bfloat16),
            jax.ShapeDtypeStruct((2 * features, features), jnp.bfloat16),
        ),
        in_specs=[hbm] * 10,
        out_specs=(vmem, vmem),
        scratch_shapes=[
            pltpu.SMEM(local_cols.shape, jnp.int32),
            pltpu.SMEM(cut_src.shape, jnp.int32),
            pltpu.SMEM(send_block.shape, jnp.int32),
            pltpu.SMEM(send_live.shape, jnp.int32),
            pltpu.VMEM(w_self.shape, jnp.bfloat16),
            pltpu.VMEM(w_neigh.shape, jnp.bfloat16),
            pltpu.VMEM(local_tiles.shape, jnp.bfloat16),
            pltpu.VMEM(cut_tiles.shape, jnp.bfloat16),
            pltpu.VMEM(blocks, jnp.bfloat16),
            pltpu.VMEM(blocks, jnp.bfloat16),
            pltpu.VMEM((n_grp * row_blocks, block, features), jnp.bfloat16),
            pltpu.VMEM((n_dom, block, features), jnp.bfloat16),
            pltpu.VMEM((n_dom, block, features), jnp.bfloat16),
            pltpu.VMEM(blocks, jnp.float32),
            pltpu.VMEM(blocks, jnp.float32),
            pltpu.VMEM((halves, 2 * features, width), jnp.float32),
            pltpu.VMEM((halves, 2 * features, width), jnp.bfloat16),
        ]
        + [pltpu.VMEM((n, r, width), jnp.bfloat16) for n, r, _, _ in sizes]
        + [pltpu.VMEM((r, width), jnp.float32) for _, r, _, _ in sizes]
        + [pltpu.VMEM((r, width), jnp.bfloat16) for _, r, _, _ in sizes]
        + [pltpu.VMEM((n, p, width), jnp.bfloat16) for _, _, n, p in sizes]
        + [
            dma((11,)),
        ]
        + [dma((n_grp,))] * 2
        + [dma((n_dom,))] * 2
        + [dma((halves, most))] * 8,
        compiler_params=pltpu.CompilerParams(
            collective_id=0, has_side_effects=True, vmem_limit_bytes=32 * 2**20
        ),
    )(
        *(
            pltpu.with_memory_space_constraint(x, pltpu.HBM)
            for x in (
                local_cols,
                cut_src,
                send_block,
                send_live,
                feats.reshape(blocks),
                w_self,
                w_neigh,
                local_tiles,
                cut_tiles,
                cotangent.reshape(blocks),
            )
        )
    )
    summed = grads.astype(jnp.float32)
    return (out.reshape(feats.shape), summed[:features], summed[features:])


def solution(mesh):
    return jax.shard_map(
        body,
        mesh=mesh,
        in_specs=(
            P(("dom", "grp"), None),
            P(),
            P(),
            P(("dom", "grp"), None, None, None),
            P(("dom", "grp"), None),
            P(("dom", "grp"), None, None, None),
            P(("dom", "grp"), None),
            P(("dom", "grp"), None),
            P(("dom", "grp"), None),
            P(("dom", "grp"), None),
        ),
        out_specs=(P(("dom", "grp"), None), P(), P()),
        check_vma=False,
    )
```
